512 devices in a mesh: ctx: 64 (over y, z), ch: 8 (over x, core).
Axes of the slice: x: 4, y: 8, z: 8, core: 2. Of those that a mesh axis runs over, the one named last changes fastest.
Arguments:
- features: bfloat16 [24576, 4096], P('ctx', 'ch'), may hold values from -6 to 6
- proj_weight: bfloat16 [4096, 4096], P('ctx', 'ch'), may hold values from -0.09375 to 0.09375
- gate_q: bfloat16 [24576, 4096], P('ctx', 'ch'), may hold values from -6 to 6
- gate_k: bfloat16 [24576, 4096], P('ctx', 'ch'), may hold values from -6 to 6
- filter_spec: float32 [2, 128, 384, 4096], P(None, 'ctx', None, 'ch'), may hold values from -6 to 6
Outputs:
- gated: bfloat16 [24576, 4096], P('ctx', 'ch')
The draws below stay inside these ranges and needn't reach their ends.
All inputs are finite; a program needn't handle non-finite values.
Results may differ from the reference program's by a relative error of at most 0.0049.
Values may be sent and summed in bfloat16 or wider, within the bound.
A program may use at most 64 MiB of HBM per device.

```python
import jax
import jax.numpy as jnp
from jax import lax

D = 4096
CHANS = 4096
TOK_DEV = 384
TOKENS = 24576
FREQ_ROWS = 128
FFT_LEN = 49152


def block_levels(rng, dims, shards, low, largest):
    def one(axis_at, blocks):
        heights = jax.random.uniform(jax.random.fold_in(jax.random.fold_in(rng, 6), axis_at), (blocks,), jnp.float32, low / len(shards), largest / len(shards))
        return jnp.repeat(jnp.exp(heights), dims[axis_at] // blocks).reshape((-1,) + (1,) * (len(dims) - axis_at - 1))

    factor_of = one(*shards[0])
    for cut in shards[1:]:
        factor_of = factor_of * one(*cut)
    return factor_of


def scatter_about(key, shape, deviation, most, shards=(), kind=jnp.bfloat16):
    gain = block_levels(key, shape, shards, -0.22, 0.18) if shards else 1.0
    array = jax.random.normal(key, shape, jnp.float32) * deviation * gain
    return jnp.minimum(jnp.maximum(array, -most), most).astype(kind)


def setup_inputs(seed: int = 0) -> dict:
    seeds = jax.random.split(jax.random.key(seed), 6)
    return {
        "features": scatter_about(seeds[0], (TOKENS, D), 1.0, 6.0, ((0, 64), (1, 8))),
        "proj_weight": scatter_about(seeds[1], (D, CHANS), D ** -0.5, 0.09375, ((0, 64), (1, 8))),
        "gate_q": scatter_about(seeds[2], (TOKENS, CHANS), 1.0, 6.0, ((0, 64), (1, 8))),
        "gate_k": scatter_about(seeds[3], (TOKENS, CHANS), 1.0, 6.0, ((0, 64), (1, 8))),
        "filter_spec": scatter_about(seeds[4], (2, FREQ_ROWS, TOK_DEV, CHANS), 1.0, 6.0, ((1, 64), (3, 8)), jnp.float32),
    }


def reference(features, proj_weight, gate_q, gate_k, filter_spec):
    projected = jnp.dot(features, proj_weight, preferred_element_type=jnp.float32)
    signal = (gate_k.astype(jnp.float32) * projected).astype(jnp.bfloat16)
    block_size = min(CHANS, 512)
    block_count = CHANS // block_size

    def one_block(block_index):
        offset = (block_index * block_size).astype(jnp.int32)
        block_signal = lax.dynamic_slice_in_dim(signal, offset, block_size, 1)
        block_spec = lax.dynamic_slice_in_dim(filter_spec, offset, block_size, 3)
        block_spec = jnp.transpose(block_spec, (0, 2, 1, 3)).reshape(2, FFT_LEN, block_size)
        padded = jnp.zeros((FFT_LEN, block_size), jnp.float32).at[:TOKENS].set(block_signal.astype(jnp.float32))
        forward = jnp.fft.fft(padded, axis=0)
        product = forward * lax.complex(block_spec[0], block_spec[1])
        return jnp.real(jnp.fft.ifft(product, axis=0))[:TOKENS]

    convolved = lax.map(one_block, jnp.arange(block_count, dtype=jnp.int32))
    convolved = jnp.transpose(convolved, (1, 0, 2)).reshape(TOKENS, CHANS)
    return (gate_q.astype(jnp.float32) * convolved).astype(jnp.bfloat16)
```

```python
import functools

import jax
import jax.numpy as jnp
import numpy as np
from jax import lax
from jax.experimental import pallas as pl
from jax.experimental.pallas import tpu as pltpu
from jax.sharding import PartitionSpec as P

BF16 = jnp.bfloat16
F32 = jnp.float32
MESH = pl.DeviceIdType.MESH
OWN = 8


def hi_lo(table):
    hi = table.astype(BF16)
    lo = (table - hi.astype(np.float64)).astype(BF16)
    return hi, lo


def tables(slabs, tok):
    rows = 2 * slabs
    k1 = np.concatenate([np.arange(0, rows, 2), np.arange(1, rows, 2)])
    ang = 2.0 * np.pi * ((k1[:, None] * np.arange(slabs)[None, :]) % rows) / rows
    fwd = np.concatenate([np.cos(ang), -np.sin(ang)], axis=0)
    inv = np.concatenate([np.cos(ang), -np.sin(ang)], axis=0).T
    first = np.concatenate(hi_lo(fwd), axis=1)
    last = np.concatenate(hi_lo(inv), axis=1)
    ang = 2.0 * np.pi * (k1[:, None] * np.arange(tok)[None, :]) / (rows * tok)
    turn = np.stack([np.cos(ang), np.sin(ang)]).astype(np.float32)
    ang = 2.0 * np.pi * ((np.arange(tok)[:, None] * np.arange(tok)[None, :]) % tok) / tok
    cos_hi, cos_lo = hi_lo(np.cos(ang))
    sin_hi, sin_lo = hi_lo(np.sin(ang))
    basis = np.stack([cos_hi, sin_hi, cos_lo, sin_lo])
    return first, last, turn, basis


def every(ref, start, count, stride):
    return jnp.concatenate(
        [ref[j, pl.ds(start, count, stride=stride), :] for j in range(ref.shape[0])], axis=1
    )


def dot(a, b):
    return jnp.dot(a, b, preferred_element_type=F32)


def kernel(
    ring, rows_x, tok, group,
    feat_in, wt_in, gq_in, gk_in, spec_in, first_in, last_in, turn_in, basis_in,
    out_ref,
    feat, wt, gq, gk, spec, first, last, turn, basis,
    spec_out, spec_got, sig_out, sig_got, ret_out, ret_got,
    acc, sig_rows, spec_rows, forward, mat, conv_rows,
    load_sem, feat_send, feat_recv, wt_send, wt_recv,
    spec_send, spec_recv, sig_send, sig_recv, ret_send, ret_recv, self_sem,
):
    slabs = ring * ring
    chans = acc.shape[1]
    half = chans // 2
    me = lax.axis_index("ctx")
    lane = lax.axis_index("ch")
    core = lax.rem(lane, 2)
    xpos = lane // 2
    ypos = me // ring
    zpos = lax.rem(me, ring)
    step_a = 1 - 2 * core
    length = 2 * slabs * tok

    def around(pos, move, size):
        return lax.rem(pos + move + size, size)

    def spot(color, p, q):
        return q * ring + p if color == 0 else p * ring + q

    loads = [
        (wt_in.at[:, pl.ds(0, half)], wt.at[0, me]),
        (wt_in.at[:, pl.ds(half, half)], wt.at[1, me]),
        (feat_in, feat.at[lane]),
        (spec_in, spec),
        (gk_in, gk),
        (gq_in, gq),
        (first_in, first),
        (last_in, last),
        (turn_in, turn),
        (basis_in, basis),
    ]
    copies = [pltpu.make_async_copy(s, d, load_sem.at[i]) for i, (s, d) in enumerate(loads)]
    for c in copies:
        c.start()

    barrier = pltpu.get_barrier_semaphore()

    def greet(k, _):
        peer = lax.rem(me + k, slabs)
        pl.semaphore_signal(barrier, inc=1, device_id=(peer, lane), device_id_type=MESH)
        return 0

    lax.fori_loop(1, slabs, greet, 0)
    partner = 2 * xpos + 1 - core
    pl.semaphore_signal(barrier, inc=1, device_id=(me, partner), device_id_type=MESH)
    greeted = slabs
    if rows_x > 1:
        for move in (1, -1):
            peer = 2 * around(xpos, move, rows_x) + core
            pl.semaphore_signal(barrier, inc=1, device_id=(me, peer), device_id_type=MESH)
        greeted += 2

    copies[3].wait()
    per = 128 // OWN
    for part in range(2):
        for odd in range(2):
            for j in range(chans // 128):
                block = spec[part, odd, :, pl.ds(128 * j, 128)].T
                spec_out[pl.ds(per * j, per), pl.ds(OWN * odd, OWN), pl.ds(tok * part, tok)] = (
                    block.reshape(per, OWN, tok).astype(BF16)
                )
    for i in (0, 1, 2):
        copies[i].wait()
    pl.semaphore_wait(barrier, greeted)

    def send_feat(slot, device):
        pltpu.make_async_remote_copy(
            src_ref=feat.at[slot], dst_ref=feat.at[slot], send_sem=feat_send,
            recv_sem=feat_recv.at[slot], device_id=(me, device), device_id_type=MESH,
        ).start()

    def wait_feat(slot):
        pltpu.make_async_copy(feat.at[slot], feat.at[slot], feat_recv.at[slot]).wait()

    def send_wt(color, slot, device):
        pltpu.make_async_remote_copy(
            src_ref=wt.at[color, slot], dst_ref=wt.at[color, slot], send_sem=wt_send,
            recv_sem=wt_recv.at[color, slot], device_id=(device, lane), device_id_type=MESH,
        ).start()

    def wait_wt(color, slot):
        pltpu.make_async_copy(wt.at[color, slot], wt.at[color, slot], wt_recv.at[color, slot]).wait()

    reach = ((step_a, ring // 2), (-step_a, ring // 2 - 1))
    place = ((zpos, ypos), (ypos, zpos))

    def along_p(color, slot, move):
        p, q = place[color]
        send_wt(color, slot, spot(color, around(p, move, ring), q))

    def along_q(color, slot, move):
        p, q = place[color]
        send_wt(color, slot, spot(color, p, around(q, move, ring)))

    for color in range(2):
        for move, far in reach:
            if far >= 1:
                along_p(color, me, move)
    for color in range(2):
        for move, far in reach:
            if far >= 1:
                along_q(color, me, move)
    reach_x = ((step_a, rows_x // 2), (-step_a, rows_x // 2 - 1))
    for move, far in reach_x:
        if far >= 1:
            send_feat(lane, 2 * around(xpos, move, rows_x) + core)
    send_feat(lane, partner)

    for k in range(1, ring // 2 + 1):
        for color in range(2):
            p, q = place[color]
            for move, far in reach:
                if k <= far:
                    slot = spot(color, around(p, -move * k, ring), q)
                    wait_wt(color, slot)
                    if k < far:
                        along_p(color, slot, move)
                    for move_q, far_q in reach:
                        if far_q >= 1:
                            along_q(color, slot, move_q)

    def pass_on(k):
        def body(j, _):
            m = (j + 1) // 2
            flip = 1 - 2 * lax.rem(j, 2)
            for color in range(2):
                p, q = place[color]
                from_p = around(p, flip * step_a * m, ring)
                for move, far in reach:
                    if k <= far:
                        slot = spot(color, from_p, around(q, -move * k, ring))
                        wait_wt(color, slot)
                        if k < far:
                            along_q(color, slot, move)
            return 0

        lax.fori_loop(0, ring, body, 0)

    for k in range(1, ring // 2 + 1):
        pass_on(k)
        for move, far in reach_x:
            if k <= far:
                slot = 2 * around(xpos, -move * k, rows_x) + core
                wait_feat(slot)
                if k < far:
                    send_feat(slot, 2 * around(xpos, move, rows_x) + core)
                send_feat(slot, partner)

    def scatter(buffer, got, send_sem, recv_sem, low, high):
        def body(k, _):
            away = lax.rem(k * 29, slabs)
            y_to = lax.rem(ypos + away // ring, ring)
            z_to = lax.rem(zpos + lax.rem(away, ring), ring)
            peer = y_to * ring + z_to
            pltpu.make_async_remote_copy(
                src_ref=buffer.at[peer], dst_ref=got.at[me], send_sem=send_sem,
                recv_sem=recv_sem.at[me], device_id=(peer, lane), device_id_type=MESH,
            ).start()
            return 0

        lax.fori_loop(low, high, body, 0)

    def collect(got, recv_sem):
        def body(k, _):
            slot = lax.rem(me + k, slabs)
            pltpu.make_async_copy(got.at[slot], got.at[slot], recv_sem.at[slot]).wait()
            return 0

        lax.fori_loop(1, slabs, body, 0)

    early = slabs // 4
    scatter(spec_out, spec_got, spec_send, spec_recv, 1, early)
    own_spec = pltpu.make_async_copy(spec_out.at[me], spec_got.at[me], self_sem.at[0])
    own_spec.start()

    for x in range(rows_x):
        wait_feat(2 * x + 1 - core)

    copies[4].wait()
    acc[...] = jnp.zeros_like(acc)
    per_feat = feat.shape[2] // wt.shape[2]

    def project(f, _):
        for color in range(2):
            block = wt[color, pl.ds(f * per_feat, per_feat)].reshape(feat.shape[2], half)
            acc[:, pl.ds(color * half, half)] += dot(feat[f], block)
        return 0

    lax.fori_loop(0, 2 * rows_x, project, 0)
    for j in range(chans // 128):
        cols = pl.ds(128 * j, 128)
        value = gk[:, cols].astype(F32) * acc[:, cols]
        sig_out[pl.ds(per * j, per)] = value.T.reshape(per, OWN, tok).astype(BF16)
    scatter(sig_out, sig_got, sig_send, sig_recv, 1, slabs)
    own_sig = pltpu.make_async_copy(sig_out.at[me], sig_got.at[me], self_sem.at[1])
    own_sig.start()
    scatter(spec_out, spec_got, spec_send, spec_recv, early, slabs)

    for i in (6, 7, 8, 9):
        copies[i].wait()
    for level in range(2):
        cosine = basis[2 * level]
        sine = basis[2 * level + 1]
        mat[level, pl.ds(0, tok), pl.ds(0, tok)] = cosine
        mat[level, pl.ds(0, tok), pl.ds(tok, tok)] = -sine
        mat[level, pl.ds(tok, tok), pl.ds(0, tok)] = sine
        mat[level, pl.ds(tok, tok), pl.ds(tok, tok)] = cosine

    own_sig.wait()
    collect(sig_got, sig_recv)
    for j in range(tok // 128):
        sig_rows[j] = sig_got[:, :, pl.ds(128 * j, 128)].astype(F32).reshape(slabs * OWN, 128)
    cos_t = turn[0]
    sin_t = turn[1]
    freqs = 2 * slabs

    def go_forward(g, _):
        pieces = []
        for u in range(group):
            x = every(sig_rows, g * group + u, slabs, OWN).astype(BF16)
            a = dot(first[...], jnp.concatenate([x, x], axis=0))
            re, im = a[:freqs], a[freqs:]
            pieces.append(
                jnp.concatenate([re * cos_t + im * sin_t, im * cos_t - re * sin_t], axis=1)
            )
        b = jnp.concatenate(pieces, axis=0)
        b_hi = b.astype(BF16)
        b_lo = (b - b_hi.astype(F32)).astype(BF16)
        full = dot(b_hi, mat[0]) + dot(b_hi, mat[1]) + dot(b_lo, mat[0])
        forward[pl.ds(g * group, group)] = full.reshape(group, freqs, 2 * tok)
        return 0

    lax.fori_loop(0, OWN // group, go_forward, 0)

    own_spec.wait()
    collect(spec_got, spec_recv)
    for j in range(2 * tok // 128):
        spec_rows[j] = (
            spec_got[:, :, pl.ds(128 * j, 128)].astype(F32).reshape(slabs * 2 * OWN, 128)
        )

    def go_back(g, _):
        pieces = []
        for u in range(group):
            c = g * group + u
            h = jnp.concatenate(
                [every(spec_rows, odd * OWN + c, slabs, 2 * OWN) for odd in range(2)],
                axis=0,
            )
            x = forward[c]
            hr, hi = h[:, :tok], h[:, tok:]
            xr, xi = x[:, :tok], x[:, tok:]
            pieces.append(
                jnp.concatenate([hr * xr - hi * xi, -(hr * xi + hi * xr)], axis=1).astype(BF16)
            )
        v = jnp.concatenate(pieces, axis=0)
        z = dot(v, mat[0]) + dot(v, mat[1])
        for u in range(group):
            zr = z[u * freqs : (u + 1) * freqs, :tok]
            zi = z[u * freqs : (u + 1) * freqs, tok:]
            both = jnp.concatenate(
                [zr * cos_t + zi * sin_t, zr * sin_t - zi * cos_t], axis=0
            ).astype(BF16)
            y = dot(last[...], jnp.concatenate([both, both], axis=0))
            y = y * (1.0 / length)
            for j in range(tok // 128):
                conv_rows[j, pl.ds(g * group + u, slabs, stride=OWN), :] = y[:, 128 * j : 128 * j + 128]
        return 0

    lax.fori_loop(0, OWN // group, go_back, 0)

    for j in range(tok // 128):
        ret_out[:, :, pl.ds(128 * j, 128)] = conv_rows[j].reshape(slabs, OWN, 128).astype(BF16)
    scatter(ret_out, ret_got, ret_send, ret_recv, 1, slabs)
    own_ret = pltpu.make_async_copy(ret_out.at[me], ret_got.at[me], self_sem.at[2])
    own_ret.start()
    copies[5].wait()
    pltpu.make_async_copy(
        wt.at[:, pl.ds(0, slabs - 1)], wt.at[:, pl.ds(0, slabs - 1)], wt_send
    ).wait()
    sent = 2 * rows_x - 1
    pltpu.make_async_copy(feat.at[pl.ds(0, sent)], feat.at[pl.ds(0, sent)], feat_send).wait()
    rest = pl.ds(0, slabs - 1)
    pltpu.make_async_copy(spec_out.at[rest], spec_out.at[rest], spec_send).wait()
    pltpu.make_async_copy(sig_out.at[rest], sig_out.at[rest], sig_send).wait()
    own_ret.wait()
    collect(ret_got, ret_recv)
    for j in range(chans // 128):
        cols = pl.ds(128 * j, 128)
        value = ret_got[pl.ds(per * j, per)].astype(F32).reshape(128, tok).T
        out_ref[:, cols] = (gq[:, cols].astype(F32) * value).astype(BF16)
    pltpu.make_async_copy(ret_out.at[rest], ret_out.at[rest], ret_send).wait()


def per_device(ring, rows_x, features, proj_weight, gate_q, gate_k, filter_spec):
    tok, feats = features.shape
    w_rows, chans = proj_weight.shape
    slabs = ring * ring
    first, last, turn, basis = tables(slabs, tok)
    any_space = pl.BlockSpec(memory_space=pl.ANY)
    freqs = 2 * slabs
    lanes = 2 * rows_x
    vm = pltpu.VMEM
    dma = pltpu.SemaphoreType.DMA
    scratch = [
        vm((lanes, tok, feats), BF16),
        vm((2, slabs, w_rows, chans // 2), BF16),
        vm((tok, chans), BF16),
        vm((tok, chans), BF16),
        vm((2, 2, tok, chans), F32),
        vm(first.shape, BF16),
        vm(last.shape, BF16),
        vm(turn.shape, F32),
        vm(basis.shape, BF16),
        vm((slabs, 2 * OWN, 2 * tok), BF16),
        vm((slabs, 2 * OWN, 2 * tok), BF16),
        vm((slabs, OWN, tok), BF16),
        vm((slabs, OWN, tok), BF16),
        vm((slabs, OWN, tok), BF16),
        vm((slabs, OWN, tok), BF16),
        vm((tok, chans), F32),
        vm((tok // 128, slabs * OWN, 128), F32),
        vm((2 * tok // 128, slabs * 2 * OWN, 128), F32),
        vm((OWN, freqs, 2 * tok), F32),
        vm((2, 2 * tok, 2 * tok), BF16),
        vm((tok // 128, slabs * OWN, 128), F32),
        dma((10,)),
        dma,
        dma((lanes,)),
        dma,
        dma((2, slabs)),
        dma,
        dma((slabs,)),
        dma,
        dma((slabs,)),
        dma,
        dma((slabs,)),
        dma((3,)),
    ]
    return pl.pallas_call(
        functools.partial(kernel, ring, rows_x, tok, 4),
        out_shape=jax.ShapeDtypeStruct((tok, chans), BF16),
        in_specs=[any_space] * 9,
        out_specs=pl.BlockSpec(memory_space=pltpu.VMEM),
        scratch_shapes=scratch,
        compiler_params=pltpu.CompilerParams(
            collective_id=0, has_side_effects=True, vmem_limit_bytes=60 * 1024 * 1024
        ),
        name="hyena",
    )(
        features, proj_weight, gate_q, gate_k, filter_spec,
        jnp.asarray(first), jnp.asarray(last), jnp.asarray(turn), jnp.asarray(basis),
    )


def solution(mesh):
    ring = int(round(mesh.shape["ctx"] ** 0.5))
    rows_x = mesh.shape["ch"] // 2
    in_specs = (
        P("ctx", "ch"),
        P("ctx", "ch"),
        P("ctx", "ch"),
        P("ctx", "ch"),
        P(None, "ctx", None, "ch"),
    )
    return jax.shard_map(
        functools.partial(per_device, ring, rows_x),
        mesh=mesh, in_specs=in_specs, out_specs=P("ctx", "ch"), check_vma=False,
    )
```

```python
import functools

import jax
import jax.numpy as jnp
import numpy as np
from jax import lax
from jax.experimental import pallas as pl
from jax.experimental.pallas import tpu as pltpu
from jax.sharding import PartitionSpec as P

BF16 = jnp.bfloat16
F32 = jnp.float32
MESH = pl.DeviceIdType.MESH
OWN = 8
HALF = OWN // 2
PACE = (2, 2, 2, 2, 2, 8)


def hi_lo(table):
    hi = table.astype(BF16)
    lo = (table - hi.astype(np.float64)).astype(BF16)
    return hi, lo


def tables(slabs, tok):
    rows = 2 * slabs
    k1 = np.concatenate([np.arange(0, rows, 2), np.arange(1, rows, 2)])
    ang = 2.0 * np.pi * ((k1[:, None] * np.arange(slabs)[None, :]) % rows) / rows
    fwd = np.concatenate([np.cos(ang), -np.sin(ang)], axis=0)
    inv = np.concatenate([np.cos(ang), -np.sin(ang)], axis=0).T
    first = np.concatenate(hi_lo(fwd), axis=1)
    last = np.concatenate(hi_lo(inv), axis=1)
    ang = 2.0 * np.pi * (k1[:, None] * np.arange(tok)[None, :]) / (rows * tok)
    turn = np.stack([np.cos(ang), np.sin(ang)]).astype(np.float32)
    ang = 2.0 * np.pi * ((np.arange(tok)[:, None] * np.arange(tok)[None, :]) % tok) / tok
    cos_hi, cos_lo = hi_lo(np.cos(ang))
    sin_hi, sin_lo = hi_lo(np.sin(ang))
    basis = np.stack([cos_hi, sin_hi, cos_lo, sin_lo])
    return first, last, turn, basis


def every(ref, start, count, stride):
    return jnp.concatenate(
        [ref[j, pl.ds(start, count, stride=stride), :] for j in range(ref.shape[0])], axis=1
    )


def dot(a, b):
    return jnp.dot(a, b, preferred_element_type=F32)


def kernel(
    ring, rows_x, tok, pace,
    feat_in, wt_in, gq_in, gk_in, spec_in, first_in, last_in, turn_in, basis_in,
    out_ref,
    feat, wt, gq, gk, spec, first, last, turn, basis,
    spec_out, spec_got, sig_out, sig_got, ret_out, ret_got,
    acc, sig_rows, spec_rows, forward, mat, conv_rows,
    load_sem, feat_send, feat_recv, wt_send, wt_recv,
    spec_send, spec_recv, sig_send, sig_recv, ret_send, ret_recv, self_sem,
):
    slabs = ring * ring
    chans = acc.shape[1]
    half = chans // 2
    me = lax.axis_index("ctx")
    lane = lax.axis_index("ch")
    core = lax.rem(lane, 2)
    xpos = lane // 2
    ypos = me // ring
    zpos = lax.rem(me, ring)
    step_a = 1 - 2 * core
    length = 2 * slabs * tok

    def around(pos, move, size):
        return lax.rem(pos + move + size, size)

    def spot(color, p, q):
        return q * ring + p if color == 0 else p * ring + q

    loads = [
        (wt_in.at[:, pl.ds(0, half)], wt.at[0, me]),
        (wt_in.at[:, pl.ds(half, half)], wt.at[1, me]),
        (feat_in, feat.at[lane]),
        (spec_in, spec),
        (gk_in, gk),
        (gq_in, gq),
        (first_in, first),
        (last_in, last),
        (turn_in, turn),
        (basis_in, basis),
    ]
    copies = [pltpu.make_async_copy(s, d, load_sem.at[i]) for i, (s, d) in enumerate(loads)]
    for c in copies:
        c.start()

    barrier = pltpu.get_barrier_semaphore()

    def greet(k, _):
        peer = lax.rem(me + k, slabs)
        pl.semaphore_signal(barrier, inc=1, device_id=(peer, lane), device_id_type=MESH)
        return 0

    lax.fori_loop(1, slabs, greet, 0)
    partner = 2 * xpos + 1 - core
    pl.semaphore_signal(barrier, inc=1, device_id=(me, partner), device_id_type=MESH)
    greeted = slabs
    if rows_x > 1:
        for move in (1, -1):
            peer = 2 * around(xpos, move, rows_x) + core
            pl.semaphore_signal(barrier, inc=1, device_id=(me, peer), device_id_type=MESH)
        greeted += 2

    copies[3].wait()
    per = 128 // OWN
    for part in range(2):
        for j in range(chans // 128):
            even, odd = (
                spec[part, b, :, pl.ds(128 * j, 128)].T.reshape(per, OWN, tok) for b in range(2)
            )
            for g in range(2):
                rows = slice(HALF * g, HALF * g + HALF)
                spec_out[g, pl.ds(per * j, per), pl.ds(OWN * part, OWN), :] = jnp.concatenate(
                    [even[:, rows], odd[:, rows]], axis=1
                ).astype(BF16)
    for i in (0, 1, 2):
        copies[i].wait()
    pl.semaphore_wait(barrier, greeted)

    def send_to(k, buffer, got, send_sem, recv_sem):
        away = lax.rem(k * 29, slabs)
        y_to = lax.rem(ypos + away // ring, ring)
        z_to = lax.rem(zpos + lax.rem(away, ring), ring)
        peer = y_to * ring + z_to
        pltpu.make_async_remote_copy(
            src_ref=buffer.at[peer], dst_ref=got.at[me], send_sem=send_sem,
            recv_sem=recv_sem.at[me], device_id=(peer, lane), device_id_type=MESH,
        ).start()

    def scatter(buffer, got, send_sem, recv_sem):
        def body(k, _):
            send_to(k, buffer, got, send_sem, recv_sem)
            return 0

        lax.fori_loop(1, slabs, body, 0)

    def send_spec(first_one, count):
        def body(n, _):
            item = first_one + n
            g = item // (slabs - 1)
            send_to(
                1 + lax.rem(item, slabs - 1), spec_out.at[g], spec_got.at[g],
                spec_send.at[g], spec_recv.at[g],
            )
            return 0

        if count > 4:
            lax.fori_loop(0, count, body, 0)
        else:
            for n in range(count):
                body(n, 0)

    def collect(got, recv_sem):
        def body(k, _):
            slot = lax.rem(me + k, slabs)
            pltpu.make_async_copy(got.at[slot], got.at[slot], recv_sem.at[slot]).wait()
            return 0

        lax.fori_loop(1, slabs, body, 0)

    def send_feat(slot, device):
        pltpu.make_async_remote_copy(
            src_ref=feat.at[slot], dst_ref=feat.at[slot], send_sem=feat_send,
            recv_sem=feat_recv.at[slot], device_id=(me, device), device_id_type=MESH,
        ).start()

    def wait_feat(slot):
        pltpu.make_async_copy(feat.at[slot], feat.at[slot], feat_recv.at[slot]).wait()

    def send_wt(color, slot, device):
        pltpu.make_async_remote_copy(
            src_ref=wt.at[color, slot], dst_ref=wt.at[color, slot], send_sem=wt_send,
            recv_sem=wt_recv.at[color, slot], device_id=(device, lane), device_id_type=MESH,
        ).start()

    def wait_wt(color, slot):
        pltpu.make_async_copy(wt.at[color, slot], wt.at[color, slot], wt_recv.at[color, slot]).wait()

    reach = ((step_a, ring // 2), (-step_a, ring // 2 - 1))
    place = ((zpos, ypos), (ypos, zpos))

    def along_p(color, slot, move):
        p, q = place[color]
        send_wt(color, slot, spot(color, around(p, move, ring), q))

    def along_q(color, slot, move):
        p, q = place[color]
        send_wt(color, slot, spot(color, p, around(q, move, ring)))

    for color in range(2):
        for move, far in reach:
            if far >= 1:
                along_p(color, me, move)
    for color in range(2):
        for move, far in reach:
            if far >= 1:
                along_q(color, me, move)
    reach_x = ((step_a, rows_x // 2), (-step_a, rows_x // 2 - 1))
    for move, far in reach_x:
        if far >= 1:
            send_feat(lane, 2 * around(xpos, move, rows_x) + core)
    send_feat(lane, partner)

    paced = 0
    for k in range(1, ring // 2 + 1):
        send_spec(paced, pace[0])
        paced += pace[0]
        for color in range(2):
            p, q = place[color]
            for move, far in reach:
                if k <= far:
                    slot = spot(color, around(p, -move * k, ring), q)
                    wait_wt(color, slot)
                    if k < far:
                        along_p(color, slot, move)
                    for move_q, far_q in reach:
                        if far_q >= 1:
                            along_q(color, slot, move_q)

    def pass_on(k, start, count):
        def body(j, _):
            send_spec(start + j * count, count)
            m = (j + 1) // 2
            flip = 1 - 2 * lax.rem(j, 2)
            for color in range(2):
                p, q = place[color]
                from_p = around(p, flip * step_a * m, ring)
                for move, far in reach:
                    if k <= far:
                        slot = spot(color, from_p, around(q, -move * k, ring))
                        wait_wt(color, slot)
                        if k < far:
                            along_q(color, slot, move)
            return 0

        lax.fori_loop(0, ring, body, 0)

    for k in range(1, ring // 2 + 1):
        pass_on(k, paced, pace[k])
        paced += ring * pace[k]
        for move, far in reach_x:
            if k <= far:
                slot = 2 * around(xpos, -move * k, rows_x) + core
                wait_feat(slot)
                if k < far:
                    send_feat(slot, 2 * around(xpos, move, rows_x) + core)
                send_feat(slot, partner)

    send_spec(paced, pace[-1])
    own_spec = [
        pltpu.make_async_copy(spec_out.at[g, me], spec_got.at[g, me], self_sem.at[g])
        for g in range(2)
    ]
    for c in own_spec:
        c.start()

    for x in range(rows_x):
        wait_feat(2 * x + 1 - core)

    copies[4].wait()
    acc[...] = jnp.zeros_like(acc)
    per_feat = feat.shape[2] // wt.shape[2]

    def project(f, _):
        for color in range(2):
            block = wt[color, pl.ds(f * per_feat, per_feat)].reshape(feat.shape[2], half)
            acc[:, pl.ds(color * half, half)] += dot(feat[f], block)
        return 0

    lax.fori_loop(0, 2 * rows_x, project, 0)
    for j in range(chans // 128):
        cols = pl.ds(128 * j, 128)
        value = gk[:, cols].astype(F32) * acc[:, cols]
        sig_out[pl.ds(per * j, per)] = value.T.reshape(per, OWN, tok).astype(BF16)
    scatter(sig_out, sig_got, sig_send, sig_recv)
    own_sig = pltpu.make_async_copy(sig_out.at[me], sig_got.at[me], self_sem.at[2])
    own_sig.start()
    send_spec(paced + pace[-1], 2 * (slabs - 1) - paced - pace[-1])

    for i in (6, 7, 8, 9):
        copies[i].wait()
    for level in range(2):
        cosine = basis[2 * level]
        sine = basis[2 * level + 1]
        mat[level, pl.ds(0, tok), pl.ds(0, tok)] = cosine
        mat[level, pl.ds(0, tok), pl.ds(tok, tok)] = -sine
        mat[level, pl.ds(tok, tok), pl.ds(0, tok)] = sine
        mat[level, pl.ds(tok, tok), pl.ds(tok, tok)] = cosine

    own_sig.wait()
    collect(sig_got, sig_recv)
    for j in range(tok // 128):
        sig_rows[j] = sig_got[:, :, pl.ds(128 * j, 128)].astype(F32).reshape(slabs * OWN, 128)
    cos_t = turn[0]
    sin_t = turn[1]
    freqs = 2 * slabs

    def go_forward(g):
        pieces = []
        for u in range(HALF):
            x = every(sig_rows, g * HALF + u, slabs, OWN).astype(BF16)
            a = dot(first[...], jnp.concatenate([x, x], axis=0))
            re, im = a[:freqs], a[freqs:]
            pieces.append(
                jnp.concatenate([re * cos_t + im * sin_t, im * cos_t - re * sin_t], axis=1)
            )
        b = jnp.concatenate(pieces, axis=0)
        b_hi = b.astype(BF16)
        b_lo = (b - b_hi.astype(F32)).astype(BF16)
        forward[...] = dot(b_hi, mat[0]) + dot(b_hi, mat[1]) + dot(b_lo, mat[0])

    def go_back(g):
        for j in range(tok // 128):
            spec_rows[j] = (
                spec_got[g, :, :, pl.ds(128 * j, 128)].astype(F32).reshape(slabs * 2 * OWN, 128)
            )
        pieces = []
        for u in range(HALF):
            hr, hi = (
                jnp.concatenate(
                    [every(spec_rows, part * OWN + b * HALF + u, slabs, 2 * OWN) for b in range(2)],
                    axis=0,
                )
                for part in range(2)
            )
            x = forward[pl.ds(u * freqs, freqs), :]
            xr, xi = x[:, :tok], x[:, tok:]
            pieces.append(
                jnp.concatenate([hr * xr - hi * xi, -(hr * xi + hi * xr)], axis=1).astype(BF16)
            )
        v = jnp.concatenate(pieces, axis=0)
        z = dot(v, mat[0]) + dot(v, mat[1])
        for u in range(HALF):
            zr = z[u * freqs : (u + 1) * freqs, :tok]
            zi = z[u * freqs : (u + 1) * freqs, tok:]
            both = jnp.concatenate(
                [zr * cos_t + zi * sin_t, zr * sin_t - zi * cos_t], axis=0
            ).astype(BF16)
            y = dot(last[...], jnp.concatenate([both, both], axis=0))
            y = y * (1.0 / length)
            for j in range(tok // 128):
                conv_rows[j, pl.ds(u, slabs, stride=HALF), :] = y[:, 128 * j : 128 * j + 128]
        for j in range(tok // 128):
            ret_out[g, :, :, pl.ds(128 * j, 128)] = (
                conv_rows[j].reshape(slabs, HALF, 128).astype(BF16)
            )

    own_ret = []
    for g in range(2):
        go_forward(g)
        own_spec[g].wait()
        collect(spec_got.at[g], spec_recv.at[g])
        go_back(g)
        scatter(ret_out.at[g], ret_got.at[g], ret_send.at[g], ret_recv.at[g])
        own_ret.append(
            pltpu.make_async_copy(ret_out.at[g, me], ret_got.at[g, me], self_sem.at[3 + g])
        )
        own_ret[g].start()

    copies[5].wait()
    pltpu.make_async_copy(
        wt.at[:, pl.ds(0, slabs - 1)], wt.at[:, pl.ds(0, slabs - 1)], wt_send
    ).wait()
    sent = 2 * rows_x - 1
    pltpu.make_async_copy(feat.at[pl.ds(0, sent)], feat.at[pl.ds(0, sent)], feat_send).wait()
    rest = pl.ds(0, slabs - 1)
    for g in range(2):
        pltpu.make_async_copy(spec_out.at[g, rest], spec_out.at[g, rest], spec_send.at[g]).wait()
    pltpu.make_async_copy(sig_out.at[rest], sig_out.at[rest], sig_send).wait()
    for g in range(2):
        own_ret[g].wait()
        collect(ret_got.at[g], ret_recv.at[g])
    for j in range(chans // 128):
        cols = pl.ds(128 * j, 128)
        value = jnp.concatenate(
            [ret_got[g, pl.ds(per * j, per)].astype(F32) for g in range(2)], axis=1
        )
        value = value.reshape(128, tok).T
        out_ref[:, cols] = (gq[:, cols].astype(F32) * value).astype(BF16)
    for g in range(2):
        pltpu.make_async_copy(ret_out.at[g, rest], ret_out.at[g, rest], ret_send.at[g]).wait()


def per_device(ring, rows_x, features, proj_weight, gate_q, gate_k, filter_spec):
    tok, feats = features.shape
    w_rows, chans = proj_weight.shape
    slabs = ring * ring
    first, last, turn, basis = tables(slabs, tok)
    any_space = pl.BlockSpec(memory_space=pl.ANY)
    freqs = 2 * slabs
    lanes = 2 * rows_x
    vm = pltpu.VMEM
    dma = pltpu.SemaphoreType.DMA
    scratch = [
        vm((lanes, tok, feats), BF16),
        vm((2, slabs, w_rows, chans // 2), BF16),
        vm((tok, chans), BF16),
        vm((tok, chans), BF16),
        vm((2, 2, tok, chans), F32),
        vm(first.shape, BF16),
        vm(last.shape, BF16),
        vm(turn.shape, F32),
        vm(basis.shape, BF16),
        vm((2, slabs, 2 * OWN, tok), BF16),
        vm((2, slabs, 2 * OWN, tok), BF16),
        vm((slabs, OWN, tok), BF16),
        vm((slabs, OWN, tok), BF16),
        vm((2, slabs, HALF, tok), BF16),
        vm((2, slabs, HALF, tok), BF16),
        vm((tok, chans), F32),
        vm((tok // 128, slabs * OWN, 128), F32),
        vm((tok // 128, slabs * 2 * OWN, 128), F32),
        vm((HALF * freqs, 2 * tok), F32),
        vm((2, 2 * tok, 2 * tok), BF16),
        vm((tok // 128, slabs * HALF, 128), F32),
        dma((10,)),
        dma,
        dma((lanes,)),
        dma,
        dma((2, slabs)),
        dma((2,)),
        dma((2, slabs)),
        dma,
        dma((slabs,)),
        dma((2,)),
        dma((2, slabs)),
        dma((5,)),
    ]
    return pl.pallas_call(
        functools.partial(kernel, ring, rows_x, tok, PACE),
        out_shape=jax.ShapeDtypeStruct((tok, chans), BF16),
        in_specs=[any_space] * 9,
        out_specs=pl.BlockSpec(memory_space=pltpu.VMEM),
        scratch_shapes=scratch,
        compiler_params=pltpu.CompilerParams(
            collective_id=0, has_side_effects=True, vmem_limit_bytes=60 * 1024 * 1024
        ),
        name="hyena",
    )(
        features, proj_weight, gate_q, gate_k, filter_spec,
        jnp.asarray(first), jnp.asarray(last), jnp.asarray(turn), jnp.asarray(basis),
    )


def solution(mesh):
    ring = int(round(mesh.shape["ctx"] ** 0.5))
    rows_x = mesh.shape["ch"] // 2
    in_specs = (
        P("ctx", "ch"),
        P("ctx", "ch"),
        P("ctx", "ch"),
        P("ctx", "ch"),
        P(None, "ctx", None, "ch"),
    )
    return jax.shard_map(
        functools.partial(per_device, ring, rows_x),
        mesh=mesh, in_specs=in_specs, out_specs=P("ctx", "ch"), check_vma=False,
    )
```

```python
import functools

import jax
import jax.numpy as jnp
import numpy as np
from jax import lax
from jax.experimental import pallas as pl
from jax.experimental.pallas import tpu as pltpu
from jax.sharding import PartitionSpec as P

BF16 = jnp.bfloat16
F32 = jnp.float32
MESH = pl.DeviceIdType.MESH
OWN = 8
HALF = OWN // 2
PACE = (2, 2, 2, 1, 1, 8)


def hi_lo(table):
    hi = table.astype(BF16)
    lo = (table - hi.astype(np.float64)).astype(BF16)
    return hi, lo


def tables(slabs, tok):
    rows = 2 * slabs
    k1 = np.concatenate([np.arange(0, rows, 2), np.arange(1, rows, 2)])
    ang = 2.0 * np.pi * ((k1[:, None] * np.arange(slabs)[None, :]) % rows) / rows
    fwd = np.concatenate([np.cos(ang), -np.sin(ang)], axis=0)
    inv = np.concatenate([np.cos(ang), -np.sin(ang)], axis=0).T
    first = np.concatenate(hi_lo(fwd), axis=1)
    last = np.concatenate(hi_lo(inv), axis=1)
    ang = 2.0 * np.pi * (k1[:, None] * np.arange(tok)[None, :]) / (rows * tok)
    turn = np.stack([np.cos(ang), np.sin(ang)]).astype(np.float32)
    ang = 2.0 * np.pi * ((np.arange(tok)[:, None] * np.arange(tok)[None, :]) % tok) / tok
    cos_hi, cos_lo = hi_lo(np.cos(ang))
    sin_hi, sin_lo = hi_lo(np.sin(ang))
    basis = np.stack([cos_hi, sin_hi, cos_lo, sin_lo])
    return first, last, turn, basis


def every(ref, start, count, stride):
    return jnp.concatenate(
        [ref[j, pl.ds(start, count, stride=stride), :] for j in range(ref.shape[0])], axis=1
    )


def dot(a, b):
    return jnp.dot(a, b, preferred_element_type=F32)


def kernel(
    ring, rows_x, tok, pace,
    feat_in, wt_in, gq_in, gk_in, spec_in, first_in, last_in, turn_in, basis_in,
    out_ref,
    feat, wt, gq, gk, spec, first, last, turn, basis,
    spec_out, spec_got, sig_out, sig_got, ret_out, ret_got,
    acc, sig_rows, spec_rows, forward, mat, conv_rows,
    load_sem, feat_send, feat_recv, wt_send, wt_recv,
    spec_send, spec_recv, sig_send, sig_recv, ret_send, ret_recv, self_sem, met,
):
    slabs = ring * ring
    chans = acc.shape[1]
    half = chans // 2
    me = lax.axis_index("ctx")
    lane = lax.axis_index("ch")
    core = lax.rem(lane, 2)
    xpos = lane // 2
    ypos = me // ring
    zpos = lax.rem(me, ring)
    step_a = 1 - 2 * core
    length = 2 * slabs * tok

    def around(pos, move, size):
        return lax.rem(pos + move + size, size)

    def spot(color, p, q):
        return q * ring + p if color == 0 else p * ring + q

    loads = [
        (wt_in.at[:, pl.ds(0, half)], wt.at[0, me]),
        (wt_in.at[:, pl.ds(half, half)], wt.at[1, me]),
        (feat_in, feat.at[lane]),
        (spec_in, spec),
        (gk_in, gk),
        (gq_in, gq),
        (first_in, first),
        (last_in, last),
        (turn_in, turn),
        (basis_in, basis),
    ]
    copies = [pltpu.make_async_copy(s, d, load_sem.at[i]) for i, (s, d) in enumerate(loads)]
    for c in copies:
        c.start()

    barrier = pltpu.get_barrier_semaphore()

    def along_z(k):
        return ypos * ring + lax.rem(zpos + k, ring)

    def along_y(k):
        return lax.rem(ypos + k, ring) * ring + zpos

    def greet(k, _):
        for peer in (along_z(k), along_y(k)):
            pl.semaphore_signal(barrier, inc=1, device_id=(peer, lane), device_id_type=MESH)
        return 0

    lax.fori_loop(1, ring, greet, 0)
    partner = 2 * xpos + 1 - core
    pl.semaphore_signal(barrier, inc=1, device_id=(me, partner), device_id_type=MESH)
    greeted = 2 * (ring - 1) + 1
    if rows_x > 1:
        for move in (1, -1):
            peer = 2 * around(xpos, move, rows_x) + core
            pl.semaphore_signal(barrier, inc=1, device_id=(me, peer), device_id_type=MESH)
        greeted += 2

    copies[3].wait()
    per = 128 // OWN
    for part in range(2):
        for j in range(chans // 128):
            even, odd = (
                spec[part, b, :, pl.ds(128 * j, 128)].T.reshape(per, OWN, tok) for b in range(2)
            )
            for g in range(2):
                rows = slice(HALF * g, HALF * g + HALF)
                spec_out[g, pl.ds(per * j, per), pl.ds(OWN * part, OWN), :] = jnp.concatenate(
                    [even[:, rows], odd[:, rows]], axis=1
                ).astype(BF16)
    for i in (0, 1, 2):
        copies[i].wait()
    pl.semaphore_wait(barrier, greeted)

    def tell(k, _):
        pl.semaphore_signal(met, inc=1, device_id=(along_z(k), lane), device_id_type=MESH)
        return 0

    lax.fori_loop(1, ring, tell, 0)

    def send_to(k, buffer, got, send_sem, recv_sem):
        away = lax.rem(k * 29, slabs)
        y_to = lax.rem(ypos + away // ring, ring)
        z_to = lax.rem(zpos + lax.rem(away, ring), ring)
        peer = y_to * ring + z_to
        pltpu.make_async_remote_copy(
            src_ref=buffer.at[peer], dst_ref=got.at[me], send_sem=send_sem,
            recv_sem=recv_sem.at[me], device_id=(peer, lane), device_id_type=MESH,
        ).start()

    def scatter(buffer, got, send_sem, recv_sem):
        def body(k, _):
            send_to(k, buffer, got, send_sem, recv_sem)
            return 0

        lax.fori_loop(1, slabs, body, 0)

    def send_spec(first_one, count):
        def body(n, _):
            item = first_one + n
            g = item // (slabs - 1)
            send_to(
                1 + lax.rem(item, slabs - 1), spec_out.at[g], spec_got.at[g],
                spec_send.at[g], spec_recv.at[g],
            )
            return 0

        if count > 4:
            lax.fori_loop(0, count, body, 0)
        else:
            for n in range(count):
                body(n, 0)

    def collect(got, recv_sem):
        def body(k, _):
            slot = lax.rem(me + k, slabs)
            pltpu.make_async_copy(got.at[slot], got.at[slot], recv_sem.at[slot]).wait()
            return 0

        lax.fori_loop(1, slabs, body, 0)

    def send_feat(slot, device):
        pltpu.make_async_remote_copy(
            src_ref=feat.at[slot], dst_ref=feat.at[slot], send_sem=feat_send,
            recv_sem=feat_recv.at[slot], device_id=(me, device), device_id_type=MESH,
        ).start()

    def wait_feat(slot):
        pltpu.make_async_copy(feat.at[slot], feat.at[slot], feat_recv.at[slot]).wait()

    def send_wt(color, slot, device):
        pltpu.make_async_remote_copy(
            src_ref=wt.at[color, slot], dst_ref=wt.at[color, slot], send_sem=wt_send,
            recv_sem=wt_recv.at[color, slot], device_id=(device, lane), device_id_type=MESH,
        ).start()

    def wait_wt(color, slot):
        pltpu.make_async_copy(wt.at[color, slot], wt.at[color, slot], wt_recv.at[color, slot]).wait()

    reach = ((step_a, ring // 2), (-step_a, ring // 2 - 1))
    place = ((zpos, ypos), (ypos, zpos))

    def along_p(color, slot, move):
        p, q = place[color]
        send_wt(color, slot, spot(color, around(p, move, ring), q))

    def along_q(color, slot, move):
        p, q = place[color]
        send_wt(color, slot, spot(color, p, around(q, move, ring)))

    for color in range(2):
        for move, far in reach:
            if far >= 1:
                along_p(color, me, move)
    for color in range(2):
        for move, far in reach:
            if far >= 1:
                along_q(color, me, move)
    reach_x = ((step_a, rows_x // 2), (-step_a, rows_x // 2 - 1))
    for move, far in reach_x:
        if far >= 1:
            send_feat(lane, 2 * around(xpos, move, rows_x) + core)
    send_feat(lane, partner)

    pl.semaphore_wait(met, ring - 1)
    paced = 0
    for k in range(1, ring // 2 + 1):
        send_spec(paced, pace[0])
        paced += pace[0]
        for color in range(2):
            p, q = place[color]
            for move, far in reach:
                if k <= far:
                    slot = spot(color, around(p, -move * k, ring), q)
                    wait_wt(color, slot)
                    if k < far:
                        along_p(color, slot, move)
                    for move_q, far_q in reach:
                        if far_q >= 1:
                            along_q(color, slot, move_q)

    def pass_on(k, start, count):
        def body(j, _):
            send_spec(start + j * count, count)
            m = (j + 1) // 2
            flip = 1 - 2 * lax.rem(j, 2)
            for color in range(2):
                p, q = place[color]
                from_p = around(p, flip * step_a * m, ring)
                for move, far in reach:
                    if k <= far:
                        slot = spot(color, from_p, around(q, -move * k, ring))
                        wait_wt(color, slot)
                        if k < far:
                            along_q(color, slot, move)
            return 0

        lax.fori_loop(0, ring, body, 0)

    per_feat = feat.shape[2] // wt.shape[2]
    last_row = around(ypos, -step_a * (ring // 2), ring)

    def project(color, low, count):
        def body(n, _):
            f = lax.rem(low + n, 2 * rows_x)
            block = wt[color, pl.ds(f * per_feat, per_feat)].reshape(feat.shape[2], half)
            acc[:, pl.ds(color * half, half)] += dot(feat[f], block)
            return 0

        lax.fori_loop(0, count, body, 0)

    for k in range(1, ring // 2 + 1):
        if k == ring // 2:
            for x in range(rows_x):
                wait_feat(2 * x + 1 - core)
            acc[...] = jnp.zeros_like(acc)
            copies[4].wait()
            project(0, last_row + 1, 2 * rows_x - 1)
        pass_on(k, paced, pace[k])
        paced += ring * pace[k]
        for move, far in reach_x:
            if k <= far:
                slot = 2 * around(xpos, -move * k, rows_x) + core
                wait_feat(slot)
                if k < far:
                    send_feat(slot, 2 * around(xpos, move, rows_x) + core)
                send_feat(slot, partner)

    send_spec(paced, pace[-1])
    own_spec = [
        pltpu.make_async_copy(spec_out.at[g, me], spec_got.at[g, me], self_sem.at[g])
        for g in range(2)
    ]
    for c in own_spec:
        c.start()

    project(0, last_row, 1)
    project(1, 0, 2 * rows_x)
    for j in range(chans // 128):
        cols = pl.ds(128 * j, 128)
        value = gk[:, cols].astype(F32) * acc[:, cols]
        sig_out[pl.ds(per * j, per)] = value.T.reshape(per, OWN, tok).astype(BF16)
    scatter(sig_out, sig_got, sig_send, sig_recv)
    own_sig = pltpu.make_async_copy(sig_out.at[me], sig_got.at[me], self_sem.at[2])
    own_sig.start()
    send_spec(paced + pace[-1], 2 * (slabs - 1) - paced - pace[-1])

    for i in (6, 7, 8, 9):
        copies[i].wait()
    for level in range(2):
        cosine = basis[2 * level]
        sine = basis[2 * level + 1]
        mat[level, pl.ds(0, tok), pl.ds(0, tok)] = cosine
        mat[level, pl.ds(0, tok), pl.ds(tok, tok)] = -sine
        mat[level, pl.ds(tok, tok), pl.ds(0, tok)] = sine
        mat[level, pl.ds(tok, tok), pl.ds(tok, tok)] = cosine

    own_sig.wait()
    collect(sig_got, sig_recv)
    for j in range(tok // 128):
        sig_rows[j] = sig_got[:, :, pl.ds(128 * j, 128)].astype(F32).reshape(slabs * OWN, 128)
    cos_t = turn[0]
    sin_t = turn[1]
    freqs = 2 * slabs

    def go_forward(g):
        pieces = []
        for u in range(HALF):
            x = every(sig_rows, g * HALF + u, slabs, OWN).astype(BF16)
            a = dot(first[...], jnp.concatenate([x, x], axis=0))
            re, im = a[:freqs], a[freqs:]
            pieces.append(
                jnp.concatenate([re * cos_t + im * sin_t, im * cos_t - re * sin_t], axis=1)
            )
        b = jnp.concatenate(pieces, axis=0)
        b_hi = b.astype(BF16)
        b_lo = (b - b_hi.astype(F32)).astype(BF16)
        forward[...] = dot(b_hi, mat[0]) + dot(b_hi, mat[1]) + dot(b_lo, mat[0])

    def go_back(g):
        for j in range(tok // 128):
            spec_rows[j] = (
                spec_got[g, :, :, pl.ds(128 * j, 128)].astype(F32).reshape(slabs * 2 * OWN, 128)
            )
        pieces = []
        for u in range(HALF):
            hr, hi = (
                jnp.concatenate(
                    [every(spec_rows, part * OWN + b * HALF + u, slabs, 2 * OWN) for b in range(2)],
                    axis=0,
                )
                for part in range(2)
            )
            x = forward[pl.ds(u * freqs, freqs), :]
            xr, xi = x[:, :tok], x[:, tok:]
            pieces.append(
                jnp.concatenate([hr * xr - hi * xi, -(hr * xi + hi * xr)], axis=1).astype(BF16)
            )
        v = jnp.concatenate(pieces, axis=0)
        z = dot(v, mat[0]) + dot(v, mat[1])
        for u in range(HALF):
            zr = z[u * freqs : (u + 1) * freqs, :tok]
            zi = z[u * freqs : (u + 1) * freqs, tok:]
            both = jnp.concatenate(
                [zr * cos_t + zi * sin_t, zr * sin_t - zi * cos_t], axis=0
            ).astype(BF16)
            y = dot(last[...], jnp.concatenate([both, both], axis=0))
            y = y * (1.0 / length)
            for j in range(tok // 128):
                conv_rows[j, pl.ds(u, slabs, stride=HALF), :] = y[:, 128 * j : 128 * j + 128]
        for j in range(tok // 128):
            ret_out[g, :, :, pl.ds(128 * j, 128)] = (
                conv_rows[j].reshape(slabs, HALF, 128).astype(BF16)
            )

    own_ret = []
    for g in range(2):
        go_forward(g)
        own_spec[g].wait()
        collect(spec_got.at[g], spec_recv.at[g])
        go_back(g)
        scatter(ret_out.at[g], ret_got.at[g], ret_send.at[g], ret_recv.at[g])
        own_ret.append(
            pltpu.make_async_copy(ret_out.at[g, me], ret_got.at[g, me], self_sem.at[3 + g])
        )
        own_ret[g].start()

    copies[5].wait()
    pltpu.make_async_copy(
        wt.at[:, pl.ds(0, slabs - 1)], wt.at[:, pl.ds(0, slabs - 1)], wt_send
    ).wait()
    sent = 2 * rows_x - 1
    pltpu.make_async_copy(feat.at[pl.ds(0, sent)], feat.at[pl.ds(0, sent)], feat_send).wait()
    rest = pl.ds(0, slabs - 1)
    for g in range(2):
        pltpu.make_async_copy(spec_out.at[g, rest], spec_out.at[g, rest], spec_send.at[g]).wait()
    pltpu.make_async_copy(sig_out.at[rest], sig_out.at[rest], sig_send).wait()
    for g in range(2):
        own_ret[g].wait()
        collect(ret_got.at[g], ret_recv.at[g])
    for j in range(chans // 128):
        cols = pl.ds(128 * j, 128)
        value = jnp.concatenate(
            [ret_got[g, pl.ds(per * j, per)].astype(F32) for g in range(2)], axis=1
        )
        value = value.reshape(128, tok).T
        out_ref[:, cols] = (gq[:, cols].astype(F32) * value).astype(BF16)
    for g in range(2):
        pltpu.make_async_copy(ret_out.at[g, rest], ret_out.at[g, rest], ret_send.at[g]).wait()


def per_device(ring, rows_x, features, proj_weight, gate_q, gate_k, filter_spec):
    tok, feats = features.shape
    w_rows, chans = proj_weight.shape
    slabs = ring * ring
    first, last, turn, basis = tables(slabs, tok)
    any_space = pl.BlockSpec(memory_space=pl.ANY)
    freqs = 2 * slabs
    lanes = 2 * rows_x
    vm = pltpu.VMEM
    dma = pltpu.SemaphoreType.DMA
    scratch = [
        vm((lanes, tok, feats), BF16),
        vm((2, slabs, w_rows, chans // 2), BF16),
        vm((tok, chans), BF16),
        vm((tok, chans), BF16),
        vm((2, 2, tok, chans), F32),
        vm(first.shape, BF16),
        vm(last.shape, BF16),
        vm(turn.shape, F32),
        vm(basis.shape, BF16),
        vm((2, slabs, 2 * OWN, tok), BF16),
        vm((2, slabs, 2 * OWN, tok), BF16),
        vm((slabs, OWN, tok), BF16),
        vm((slabs, OWN, tok), BF16),
        vm((2, slabs, HALF, tok), BF16),
        vm((2, slabs, HALF, tok), BF16),
        vm((tok, chans), F32),
        vm((tok // 128, slabs * OWN, 128), F32),
        vm((tok // 128, slabs * 2 * OWN, 128), F32),
        vm((HALF * freqs, 2 * tok), F32),
        vm((2, 2 * tok, 2 * tok), BF16),
        vm((tok // 128, slabs * HALF, 128), F32),
        dma((10,)),
        dma,
        dma((lanes,)),
        dma,
        dma((2, slabs)),
        dma((2,)),
        dma((2, slabs)),
        dma,
        dma((slabs,)),
        dma((2,)),
        dma((2, slabs)),
        dma((5,)),
        pltpu.SemaphoreType.REGULAR,
    ]
    return pl.pallas_call(
        functools.partial(kernel, ring, rows_x, tok, PACE),
        out_shape=jax.ShapeDtypeStruct((tok, chans), BF16),
        in_specs=[any_space] * 9,
        out_specs=pl.BlockSpec(memory_space=pltpu.VMEM),
        scratch_shapes=scratch,
        compiler_params=pltpu.CompilerParams(
            collective_id=0, has_side_effects=True, vmem_limit_bytes=60 * 1024 * 1024
        ),
        name="hyena",
    )(
        features, proj_weight, gate_q, gate_k, filter_spec,
        jnp.asarray(first), jnp.asarray(last), jnp.asarray(turn), jnp.asarray(basis),
    )


def solution(mesh):
    ring = int(round(mesh.shape["ctx"] ** 0.5))
    rows_x = mesh.shape["ch"] // 2
    in_specs = (
        P("ctx", "ch"),
        P("ctx", "ch"),
        P("ctx", "ch"),
        P("ctx", "ch"),
        P(None, "ctx", None, "ch"),
    )
    return jax.shard_map(
        functools.partial(per_device, ring, rows_x),
        mesh=mesh, in_specs=in_specs, out_specs=P("ctx", "ch"), check_vma=False,
    )
```

```python
import functools

import jax
import jax.numpy as jnp
import numpy as np
from jax import lax
from jax.experimental import pallas as pl
from jax.experimental.pallas import tpu as pltpu
from jax.sharding import PartitionSpec as P

BF16 = jnp.bfloat16
F32 = jnp.float32
MESH = pl.DeviceIdType.MESH
OWN = 8
HALF = OWN // 2
PACE = (2, 2, 2, 1, 1, 8)


def hi_lo(table):
    hi = table.astype(BF16)
    lo = (table - hi.astype(np.float64)).astype(BF16)
    return hi, lo


def tables(slabs, tok):
    rows = 2 * slabs
    k1 = np.concatenate([np.arange(0, rows, 2), np.arange(1, rows, 2)])
    ang = 2.0 * np.pi * ((k1[:, None] * np.arange(slabs)[None, :]) % rows) / rows
    fwd = np.concatenate([np.cos(ang), -np.sin(ang)], axis=0)
    inv = np.concatenate([np.cos(ang), -np.sin(ang)], axis=0).T
    first = np.concatenate(hi_lo(fwd), axis=1)
    last = np.concatenate(hi_lo(inv), axis=1)
    ang = 2.0 * np.pi * (k1[:, None] * np.arange(tok)[None, :]) / (rows * tok)
    turn = np.stack([np.cos(ang), np.sin(ang)]).astype(np.float32)
    ang = 2.0 * np.pi * ((np.arange(tok)[:, None] * np.arange(tok)[None, :]) % tok) / tok
    cos_hi, cos_lo = hi_lo(np.cos(ang))
    sin_hi, sin_lo = hi_lo(np.sin(ang))
    basis = np.stack([cos_hi, sin_hi, cos_lo, sin_lo])
    return first, last, turn, basis


def every(ref, start, count, stride):
    return jnp.concatenate(
        [ref[j, pl.ds(start, count, stride=stride), :] for j in range(ref.shape[0])], axis=1
    )


def dot(a, b):
    return jnp.dot(a, b, preferred_element_type=F32)


def kernel(
    ring, rows_x, tok, pace,
    feat_in, wt_in, gq_in, gk_in, spec_in, first_in, last_in, turn_in, basis_in,
    out_ref,
    feat, wt, gq, gk, spec, first, last, turn, basis,
    spec_out, spec_got, sig_out, sig_got, ret_out, ret_got,
    acc, sig_rows, spec_rows, forward, mat, conv_rows,
    load_sem, feat_send, feat_recv, wt_send, wt_recv,
    spec_send, spec_recv, sig_send, sig_recv, ret_send, ret_recv, self_sem, met,
):
    slabs = ring * ring
    chans = acc.shape[1]
    half = chans // 2
    me = lax.axis_index("ctx")
    lane = lax.axis_index("ch")
    core = lax.rem(lane, 2)
    xpos = lane // 2
    ypos = me // ring
    zpos = lax.rem(me, ring)
    step_a = 1 - 2 * core
    length = 2 * slabs * tok

    def around(pos, move, size):
        return lax.rem(pos + move + size, size)

    def spot(color, p, q):
        return q * ring + p if color == 0 else p * ring + q

    loads = [
        (wt_in.at[:, pl.ds(0, half)], wt.at[0, ypos * ring + zpos]),
        (wt_in.at[:, pl.ds(half, half)], wt.at[1, zpos * ring + ypos]),
        (feat_in, feat.at[lane]),
        (spec_in, spec),
        (gk_in, gk),
        (gq_in, gq),
        (first_in, first),
        (last_in, last),
        (turn_in, turn),
        (basis_in, basis),
    ]
    copies = [pltpu.make_async_copy(s, d, load_sem.at[i]) for i, (s, d) in enumerate(loads)]
    for c in copies:
        c.start()

    barrier = pltpu.get_barrier_semaphore()

    def along_z(k):
        return ypos * ring + lax.rem(zpos + k, ring)

    def along_y(k):
        return lax.rem(ypos + k, ring) * ring + zpos

    def greet(k, _):
        for peer in (along_z(k), along_y(k)):
            pl.semaphore_signal(barrier, inc=1, device_id=(peer, lane), device_id_type=MESH)
        return 0

    lax.fori_loop(1, ring, greet, 0)
    partner = 2 * xpos + 1 - core
    pl.semaphore_signal(barrier, inc=1, device_id=(me, partner), device_id_type=MESH)
    greeted = 2 * (ring - 1) + 1
    if rows_x > 1:
        for move in (1, -1):
            peer = 2 * around(xpos, move, rows_x) + core
            pl.semaphore_signal(barrier, inc=1, device_id=(me, peer), device_id_type=MESH)
        greeted += 2

    copies[3].wait()
    per = 128 // OWN
    for part in range(2):
        for j in range(chans // 128):
            even, odd = (
                spec[part, b, :, pl.ds(128 * j, 128)].T.reshape(per, OWN, tok) for b in range(2)
            )
            for g in range(2):
                rows = slice(HALF * g, HALF * g + HALF)
                spec_out[g, pl.ds(per * j, per), pl.ds(OWN * part, OWN), :] = jnp.concatenate(
                    [even[:, rows], odd[:, rows]], axis=1
                ).astype(BF16)
    for i in (0, 1, 2):
        copies[i].wait()
    pl.semaphore_wait(barrier, greeted)

    def tell(k, _):
        pl.semaphore_signal(met, inc=1, device_id=(along_z(k), lane), device_id_type=MESH)
        return 0

    lax.fori_loop(1, ring, tell, 0)

    def send_to(k, buffer, got, send_sem, recv_sem):
        away = lax.rem(k * 29, slabs)
        y_to = lax.rem(ypos + away // ring, ring)
        z_to = lax.rem(zpos + lax.rem(away, ring), ring)
        peer = y_to * ring + z_to
        pltpu.make_async_remote_copy(
            src_ref=buffer.at[peer], dst_ref=got.at[me], send_sem=send_sem,
            recv_sem=recv_sem.at[me], device_id=(peer, lane), device_id_type=MESH,
        ).start()

    def scatter(buffer, got, send_sem, recv_sem):
        def body(k, _):
            send_to(k, buffer, got, send_sem, recv_sem)
            return 0

        lax.fori_loop(1, slabs, body, 0)

    def send_spec(first_one, count):
        def body(n, _):
            item = first_one + n
            g = item // (slabs - 1)
            send_to(
                1 + lax.rem(item, slabs - 1), spec_out.at[g], spec_got.at[g],
                spec_send.at[g], spec_recv.at[g],
            )
            return 0

        if count > 4:
            lax.fori_loop(0, count, body, 0)
        else:
            for n in range(count):
                body(n, 0)

    def collect(got, recv_sem):
        def body(k, _):
            slot = lax.rem(me + k, slabs)
            pltpu.make_async_copy(got.at[slot], got.at[slot], recv_sem.at[slot]).wait()
            return 0

        lax.fori_loop(1, slabs, body, 0)

    def send_feat(slot, device):
        pltpu.make_async_remote_copy(
            src_ref=feat.at[slot], dst_ref=feat.at[slot], send_sem=feat_send,
            recv_sem=feat_recv.at[slot], device_id=(me, device), device_id_type=MESH,
        ).start()

    def wait_feat(slot):
        pltpu.make_async_copy(feat.at[slot], feat.at[slot], feat_recv.at[slot]).wait()

    def send_wt(color, slot, device):
        pltpu.make_async_remote_copy(
            src_ref=wt.at[color, slot], dst_ref=wt.at[color, slot], send_sem=wt_send,
            recv_sem=wt_recv.at[color, slot], device_id=(device, lane), device_id_type=MESH,
        ).start()

    def wait_wt(color, slot):
        pltpu.make_async_copy(wt.at[color, slot], wt.at[color, slot], wt_recv.at[color, slot]).wait()

    reach = ((step_a, ring // 2), (-step_a, ring // 2 - 1))
    place = ((zpos, ypos), (ypos, zpos))

    def along_p(color, slot, move):
        p, q = place[color]
        send_wt(color, slot, spot(color, around(p, move, ring), q))

    def along_q(color, slot, move):
        p, q = place[color]
        send_wt(color, slot, spot(color, p, around(q, move, ring)))

    for color in range(2):
        for move, far in reach:
            if far >= 1:
                along_p(color, place[color][1] * ring + place[color][0], move)
    for color in range(2):
        for move, far in reach:
            if far >= 1:
                along_q(color, place[color][1] * ring + place[color][0], move)
    reach_x = ((step_a, rows_x // 2), (-step_a, rows_x // 2 - 1))
    for move, far in reach_x:
        if far >= 1:
            send_feat(lane, 2 * around(xpos, move, rows_x) + core)
    send_feat(lane, partner)

    pl.semaphore_wait(met, ring - 1)
    paced = 0
    for k in range(1, ring // 2 + 1):
        send_spec(paced, pace[0])
        paced += pace[0]
        for color in range(2):
            p, q = place[color]
            for move, far in reach:
                if k <= far:
                    slot = q * ring + around(p, -move * k, ring)
                    wait_wt(color, slot)
                    if k < far:
                        along_p(color, slot, move)
                    for move_q, far_q in reach:
                        if far_q >= 1:
                            along_q(color, slot, move_q)

    def pair(color, low):
        return wt.at[color, pl.ds(low, 2)]

    def pass_on(k, start, count):
        def body(j, _):
            send_spec(start + j * 2 * count, 2 * count)
            for color in range(2):
                p, q = place[color]
                first_p = 2 * lax.rem(p // 2 + j, ring // 2)
                for move, far in reach:
                    if k <= far:
                        low = around(q, -move * k, ring) * ring + first_p
                        if k == 1:
                            wait_wt(color, low)
                            wait_wt(color, low + 1)
                        else:
                            pltpu.make_async_copy(
                                pair(color, low), pair(color, low), wt_recv.at[color, low]
                            ).wait()
                        if k < far:
                            pltpu.make_async_remote_copy(
                                src_ref=pair(color, low), dst_ref=pair(color, low),
                                send_sem=wt_send, recv_sem=wt_recv.at[color, low],
                                device_id=(spot(color, p, around(q, move, ring)), lane),
                                device_id_type=MESH,
                            ).start()
            return 0

        lax.fori_loop(0, ring // 2, body, 0)

    per_feat = feat.shape[2] // wt.shape[2]
    last_row = around(ypos, -step_a * (ring // 2), ring)

    def project(color, low, count):
        def body(n, _):
            f = lax.rem(low + n, 2 * rows_x)
            if color == 0:
                block = wt[0, pl.ds(f * per_feat, per_feat)].reshape(feat.shape[2], half)
            else:
                block = jnp.concatenate([wt[1, z * ring + f] for z in range(ring)], axis=0)
            acc[:, pl.ds(color * half, half)] += dot(feat[f], block)
            return 0

        lax.fori_loop(0, count, body, 0)

    for k in range(1, ring // 2 + 1):
        if k == ring // 2:
            for x in range(rows_x):
                wait_feat(2 * x + 1 - core)
            acc[...] = jnp.zeros_like(acc)
            copies[4].wait()
            project(0, last_row + 1, 2 * rows_x - 1)
        pass_on(k, paced, pace[k])
        paced += ring * pace[k]
        for move, far in reach_x:
            if k <= far:
                slot = 2 * around(xpos, -move * k, rows_x) + core
                wait_feat(slot)
                if k < far:
                    send_feat(slot, 2 * around(xpos, move, rows_x) + core)
                send_feat(slot, partner)

    send_spec(paced, pace[-1])
    own_spec = [
        pltpu.make_async_copy(spec_out.at[g, me], spec_got.at[g, me], self_sem.at[g])
        for g in range(2)
    ]
    for c in own_spec:
        c.start()

    project(0, last_row, 1)
    project(1, 0, 2 * rows_x)
    for j in range(chans // 128):
        cols = pl.ds(128 * j, 128)
        value = gk[:, cols].astype(F32) * acc[:, cols]
        sig_out[pl.ds(per * j, per)] = value.T.reshape(per, OWN, tok).astype(BF16)
    scatter(sig_out, sig_got, sig_send, sig_recv)
    own_sig = pltpu.make_async_copy(sig_out.at[me], sig_got.at[me], self_sem.at[2])
    own_sig.start()
    send_spec(paced + pace[-1], 2 * (slabs - 1) - paced - pace[-1])

    for i in (6, 7, 8, 9):
        copies[i].wait()
    for level in range(2):
        cosine = basis[2 * level]
        sine = basis[2 * level + 1]
        mat[level, pl.ds(0, tok), pl.ds(0, tok)] = cosine
        mat[level, pl.ds(0, tok), pl.ds(tok, tok)] = -sine
        mat[level, pl.ds(tok, tok), pl.ds(0, tok)] = sine
        mat[level, pl.ds(tok, tok), pl.ds(tok, tok)] = cosine

    own_sig.wait()
    collect(sig_got, sig_recv)
    for j in range(tok // 128):
        sig_rows[j] = sig_got[:, :, pl.ds(128 * j, 128)].astype(F32).reshape(slabs * OWN, 128)
    cos_t = turn[0]
    sin_t = turn[1]
    freqs = 2 * slabs

    def go_forward(g):
        pieces = []
        for u in range(HALF):
            x = every(sig_rows, g * HALF + u, slabs, OWN).astype(BF16)
            a = dot(first[...], jnp.concatenate([x, x], axis=0))
            re, im = a[:freqs], a[freqs:]
            pieces.append(
                jnp.concatenate([re * cos_t + im * sin_t, im * cos_t - re * sin_t], axis=1)
            )
        b = jnp.concatenate(pieces, axis=0)
        b_hi = b.astype(BF16)
        b_lo = (b - b_hi.astype(F32)).astype(BF16)
        forward[...] = dot(b_hi, mat[0]) + dot(b_hi, mat[1]) + dot(b_lo, mat[0])

    def go_back(g):
        for j in range(tok // 128):
            spec_rows[j] = (
                spec_got[g, :, :, pl.ds(128 * j, 128)].astype(F32).reshape(slabs * 2 * OWN, 128)
            )
        pieces = []
        for u in range(HALF):
            hr, hi = (
                jnp.concatenate(
                    [every(spec_rows, part * OWN + b * HALF + u, slabs, 2 * OWN) for b in range(2)],
                    axis=0,
                )
                for part in range(2)
            )
            x = forward[pl.ds(u * freqs, freqs), :]
            xr, xi = x[:, :tok], x[:, tok:]
            pieces.append(
                jnp.concatenate([hr * xr - hi * xi, -(hr * xi + hi * xr)], axis=1).astype(BF16)
            )
        v = jnp.concatenate(pieces, axis=0)
        z = dot(v, mat[0]) + dot(v, mat[1])
        for u in range(HALF):
            zr = z[u * freqs : (u + 1) * freqs, :tok]
            zi = z[u * freqs : (u + 1) * freqs, tok:]
            both = jnp.concatenate(
                [zr * cos_t + zi * sin_t, zr * sin_t - zi * cos_t], axis=0
            ).astype(BF16)
            y = dot(last[...], jnp.concatenate([both, both], axis=0))
            y = y * (1.0 / length)
            for j in range(tok // 128):
                conv_rows[j, pl.ds(u, slabs, stride=HALF), :] = y[:, 128 * j : 128 * j + 128]
        for j in range(tok // 128):
            ret_out[g, :, :, pl.ds(128 * j, 128)] = (
                conv_rows[j].reshape(slabs, HALF, 128).astype(BF16)
            )

    own_ret = []
    for g in range(2):
        go_forward(g)
        own_spec[g].wait()
        collect(spec_got.at[g], spec_recv.at[g])
        go_back(g)
        scatter(ret_out.at[g], ret_got.at[g], ret_send.at[g], ret_recv.at[g])
        own_ret.append(
            pltpu.make_async_copy(ret_out.at[g, me], ret_got.at[g, me], self_sem.at[3 + g])
        )
        own_ret[g].start()

    copies[5].wait()
    pltpu.make_async_copy(
        wt.at[:, pl.ds(0, slabs - 1)], wt.at[:, pl.ds(0, slabs - 1)], wt_send
    ).wait()
    sent = 2 * rows_x - 1
    pltpu.make_async_copy(feat.at[pl.ds(0, sent)], feat.at[pl.ds(0, sent)], feat_send).wait()
    rest = pl.ds(0, slabs - 1)
    for g in range(2):
        pltpu.make_async_copy(spec_out.at[g, rest], spec_out.at[g, rest], spec_send.at[g]).wait()
    pltpu.make_async_copy(sig_out.at[rest], sig_out.at[rest], sig_send).wait()
    for g in range(2):
        own_ret[g].wait()
        collect(ret_got.at[g], ret_recv.at[g])
    for j in range(chans // 128):
        cols = pl.ds(128 * j, 128)
        value = jnp.concatenate(
            [ret_got[g, pl.ds(per * j, per)].astype(F32) for g in range(2)], axis=1
        )
        value = value.reshape(128, tok).T
        out_ref[:, cols] = (gq[:, cols].astype(F32) * value).astype(BF16)
    for g in range(2):
        pltpu.make_async_copy(ret_out.at[g, rest], ret_out.at[g, rest], ret_send.at[g]).wait()


def per_device(ring, rows_x, features, proj_weight, gate_q, gate_k, filter_spec):
    tok, feats = features.shape
    w_rows, chans = proj_weight.shape
    slabs = ring * ring
    first, last, turn, basis = tables(slabs, tok)
    any_space = pl.BlockSpec(memory_space=pl.ANY)
    freqs = 2 * slabs
    lanes = 2 * rows_x
    vm = pltpu.VMEM
    dma = pltpu.SemaphoreType.DMA
    scratch = [
        vm((lanes, tok, feats), BF16),
        vm((2, slabs, w_rows, chans // 2), BF16),
        vm((tok, chans), BF16),
        vm((tok, chans), BF16),
        vm((2, 2, tok, chans), F32),
        vm(first.shape, BF16),
        vm(last.shape, BF16),
        vm(turn.shape, F32),
        vm(basis.shape, BF16),
        vm((2, slabs, 2 * OWN, tok), BF16),
        vm((2, slabs, 2 * OWN, tok), BF16),
        vm((slabs, OWN, tok), BF16),
        vm((slabs, OWN, tok), BF16),
        vm((2, slabs, HALF, tok), BF16),
        vm((2, slabs, HALF, tok), BF16),
        vm((tok, chans), F32),
        vm((tok // 128, slabs * OWN, 128), F32),
        vm((tok // 128, slabs * 2 * OWN, 128), F32),
        vm((HALF * freqs, 2 * tok), F32),
        vm((2, 2 * tok, 2 * tok), BF16),
        vm((tok // 128, slabs * HALF, 128), F32),
        dma((10,)),
        dma,
        dma((lanes,)),
        dma,
        dma((2, slabs)),
        dma((2,)),
        dma((2, slabs)),
        dma,
        dma((slabs,)),
        dma((2,)),
        dma((2, slabs)),
        dma((5,)),
        pltpu.SemaphoreType.REGULAR,
    ]
    return pl.pallas_call(
        functools.partial(kernel, ring, rows_x, tok, PACE),
        out_shape=jax.ShapeDtypeStruct((tok, chans), BF16),
        in_specs=[any_space] * 9,
        out_specs=pl.BlockSpec(memory_space=pltpu.VMEM),
        scratch_shapes=scratch,
        compiler_params=pltpu.CompilerParams(
            collective_id=0, has_side_effects=True, vmem_limit_bytes=60 * 1024 * 1024
        ),
        name="hyena",
    )(
        features, proj_weight, gate_q, gate_k, filter_spec,
        jnp.asarray(first), jnp.asarray(last), jnp.asarray(turn), jnp.asarray(basis),
    )


def solution(mesh):
    ring = int(round(mesh.shape["ctx"] ** 0.5))
    rows_x = mesh.shape["ch"] // 2
    in_specs = (
        P("ctx", "ch"),
        P("ctx", "ch"),
        P("ctx", "ch"),
        P("ctx", "ch"),
        P(None, "ctx", None, "ch"),
    )
    return jax.shard_map(
        functools.partial(per_device, ring, rows_x),
        mesh=mesh, in_specs=in_specs, out_specs=P("ctx", "ch"), check_vma=False,
    )
```
